32 devices in a mesh: ent: 8 (over z, y), rep: 4 (over x, core).
Axes of the slice: x: 2, y: 2, z: 4, core: 2. Of those that a mesh axis runs over, the one named last changes fastest.
Arguments:
- memory: bfloat16 [16384, 512], P('ent'), may hold values from -6 to 6
- edge_features: bfloat16 [12288, 128], P(('ent', 'rep')), may hold values from -6 to 6
- source: int32 [12288], P(('ent', 'rep')), may hold values from 0 to 16383, as said below
- target: int32 [12288], P(('ent', 'rep')), may hold values from 0 to 16383, as said below
- cotangent: bfloat16 [12288, 512], P(('ent', 'rep')), may hold values from -6 to 6
- w_first: bfloat16 [1152, 512], replicated, may hold values from -0.1875 to 0.1875
- w_second: bfloat16 [512, 512], replicated, may hold values from -0.25 to 0.25
- w_input: bfloat16 [512, 1536], replicated, may hold values from -0.25 to 0.25
- w_hidden: bfloat16 [512, 1536], replicated, may hold values from -0.25 to 0.25
Outputs:
- memory_grad: float32 [16384, 512], P('ent', 'rep')
- first_grad: float32 [1152, 512], P('ent')
- second_grad: float32 [512, 512], P('ent')
- input_grad: float32 [512, 1536], P('ent')
- hidden_grad: float32 [512, 1536], P('ent')
The draws below stay inside these ranges and needn't reach their ends.
Inputs may be any that keep to these rules, and one draw needn't show every extreme that they name: `source`: entity ids; an entity is a hub when its id modulo 2048 is below 8, and its owner is its id divided by 2048. In each aligned block of 384 events (the events of one device), sources and targets taken together hold exactly 192 hub endpoints; no owner gets more than 144 non-hub endpoints or more than 240 endpoints in all from one block, and in every draw one owner gets exactly 144 non-hub endpoints and 240 in all from every block. `target`: entity ids under the same rules, counted together with source.
All inputs are finite; a program needn't handle non-finite values.
Results may differ from the reference program's by a relative error of at most 0.0057.
Values may be sent and summed in bfloat16 or wider, within the bound.
No kernel may reach another device: no remote copies, remote signals or barrier semaphores. Data moves between devices by JAX's collectives and lax.ppermute only.
A program may use at most 128 MiB of HBM per device.

```python
import math
import jax
import jax.numpy as jnp
from jax import lax

DIM = 512
EDGE = 128
HUB_DEV = 8
E_DEV = 384
ENT_DEV = 2048
OWNERS = 8
BATCHES = 32
EVENTS = 12288
ENTITIES = 16384
IN_ROWS = 1152
HUB_REQ = 192
NONHUB = 576
CAP_REST = 144
CAP_HUB = 96


def endpoint_table(key):
    shared = jax.random.fold_in(key, 7)
    star_key, weight_key = jax.random.split(shared)
    busiest = jax.random.randint(star_key, (), 0, OWNERS)
    penalty = jax.random.randint(weight_key, (OWNERS,), 0, 4)
    rest_slots = OWNERS * CAP_REST
    hub_slots = OWNERS * CAP_HUB

    def one_block(block_id):
        block_key = jax.random.fold_in(jax.random.fold_in(key, 11), block_id)
        block_keys = jax.random.split(block_key, 5)
        slot_ids = jnp.arange(rest_slots, dtype=jnp.int32)
        slot_owner = slot_ids // CAP_REST
        rest_noise = jax.random.randint(block_keys[0], (rest_slots,), 1, 65537)
        ranking = jnp.where(slot_owner == busiest, 0, rest_noise) * rest_slots + slot_ids
        chosen = jnp.argsort(ranking, stable=True)[:NONHUB].astype(jnp.int32)
        rest_rows = jax.random.randint(block_keys[1], (NONHUB,), HUB_DEV, ENT_DEV)
        rest_ids = chosen // CAP_REST * ENT_DEV + rest_rows
        hub_slot_ids = jnp.arange(hub_slots, dtype=jnp.int32)
        hub_owner = hub_slot_ids // CAP_HUB
        hub_noise = penalty[hub_owner] * 4096 + jax.random.randint(block_keys[2], (hub_slots,), 1, 4097)
        hub_rank = jnp.where(hub_owner == busiest, 0, hub_noise) * hub_slots + hub_slot_ids
        hub_chosen = jnp.argsort(hub_rank, stable=True)[:HUB_REQ].astype(jnp.int32)
        hub_rows = jax.random.randint(block_keys[3], (HUB_REQ,), 0, HUB_DEV)
        hub_ids = hub_chosen // CAP_HUB * ENT_DEV + hub_rows
        endpoints = jnp.concatenate([rest_ids, hub_ids]).astype(jnp.int32)
        return jax.random.permutation(block_keys[4], endpoints)
    return jax.vmap(one_block)(jnp.arange(BATCHES, dtype=jnp.int32))


def draw_source(key, part):
    return endpoint_table(key)[:, :E_DEV].reshape(EVENTS)


def draw_target(key, part):
    return endpoint_table(key)[:, E_DEV:].reshape(EVENTS)


def level_of(rng, dims, cuts, smallest, top_value):
    gain = 1.0
    for position, blocks in cuts:
        draws = jax.random.uniform(jax.random.fold_in(jax.random.fold_in(rng, 6), position), (blocks,), jnp.float32, smallest / len(cuts), top_value / len(cuts))
        gain = gain * jnp.repeat(jnp.exp(draws), dims[position] // blocks).reshape((-1,) + (1,) * (len(dims) - 1 - position))
    return gain


def normal_values(own_key, dims, width, bound, cuts=(), kind=jnp.bfloat16):
    loudness = level_of(own_key, dims, cuts, -0.22, 0.18) if cuts else 1.0
    result = jax.random.normal(own_key, dims, jnp.float32) * width * loudness
    return jnp.minimum(jnp.maximum(result, -bound), bound).astype(kind)


def setup_inputs(seed: int = 0) -> dict:
    arg_keys = jax.random.split(jax.random.key(seed), 10)
    memory = normal_values(arg_keys[0], (ENTITIES, DIM), 1.0, 6.0, ((0, 8),))
    edge_features = normal_values(arg_keys[1], (EVENTS, EDGE), 1.0, 6.0, ((0, 32),))
    source = draw_source(jax.random.fold_in(arg_keys[9], 71), 0)
    target = draw_target(jax.random.fold_in(arg_keys[9], 71), 0)
    cotangent = normal_values(arg_keys[4], (EVENTS, DIM), 1.0, 6.0, ((0, 32),))
    w_first = normal_values(arg_keys[5], (IN_ROWS, DIM), IN_ROWS ** -0.5, 0.1875)
    w_second = normal_values(arg_keys[6], (DIM, DIM), DIM ** -0.5, 0.25)
    w_input = normal_values(arg_keys[7], (DIM, 3 * DIM), DIM ** -0.5, 0.25)
    w_hidden = normal_values(arg_keys[8], (DIM, 3 * DIM), DIM ** -0.5, 0.25)
    return dict(memory=memory, edge_features=edge_features, source=source, target=target, cotangent=cotangent, w_first=w_first, w_second=w_second, w_input=w_input, w_hidden=w_hidden)


def contract_last(left, right):
    return lax.dot_general(left, right, (((1,), (1,)), ((), ())), preferred_element_type=jnp.float32)

def event_backward(mem_src, mem_dst, edge_rows, cot_rows, w_first, w_second, w_input, w_hidden):
    mem_width = mem_src.shape[1]
    inputs = jnp.concatenate([mem_src, mem_dst, edge_rows], axis=1)
    pre_hidden = jnp.dot(inputs, w_first, preferred_element_type=jnp.float32)
    hidden = jax.nn.silu(pre_hidden).astype(jnp.bfloat16)
    message = jnp.dot(hidden, w_second, preferred_element_type=jnp.float32).astype(jnp.bfloat16)
    gate_in = jnp.dot(message, w_input, preferred_element_type=jnp.float32)
    gate_mem = jnp.dot(mem_src, w_hidden, preferred_element_type=jnp.float32)
    reset_gate = jax.nn.sigmoid(gate_in[:, :mem_width] + gate_mem[:, :mem_width])
    update = jax.nn.sigmoid(gate_in[:, mem_width:2 * mem_width] + gate_mem[:, mem_width:2 * mem_width])
    mem_cand = gate_mem[:, 2 * mem_width:]
    candidate = jnp.tanh(gate_in[:, 2 * mem_width:] + reset_gate * mem_cand)
    upstream = cot_rows.astype(jnp.float32)
    pre_cand = upstream * (1.0 - update) * (1.0 - candidate * candidate)
    pre_reset = pre_cand * mem_cand * reset_gate * (1.0 - reset_gate)
    pre_update = upstream * (mem_src.astype(jnp.float32) - candidate) * update * (1.0 - update)
    d_gate_in = jnp.concatenate([pre_reset, pre_update, pre_cand], axis=1).astype(jnp.bfloat16)
    d_gate_mem = jnp.concatenate([pre_reset, pre_update, pre_cand * reset_gate], axis=1).astype(jnp.bfloat16)
    d_message = contract_last(d_gate_in, w_input).astype(jnp.bfloat16)
    back_hidden = contract_last(d_message, w_second)
    sigma_pre = jax.nn.sigmoid(pre_hidden)
    d_pre = (back_hidden * sigma_pre * (1.0 + pre_hidden * (1.0 - sigma_pre))).astype(jnp.bfloat16)
    d_inputs = contract_last(d_pre, w_first[:2 * mem_width])
    via_memory = contract_last(d_gate_mem, w_hidden)
    d_source = upstream * update + via_memory + d_inputs[:, :mem_width]
    d_target = d_inputs[:, mem_width:]
    saved_rows = (inputs, d_pre, hidden, d_message, message, d_gate_in, d_gate_mem)
    return (d_source, d_target, saved_rows)

def reference(memory, edge_features, source, target, cotangent, w_first, w_second, w_input, w_hidden):
    mem_width = memory.shape[1]

    def scan_step(carried, block_rows):
        mem_grad, grad_first, grad_rest = carried
        edge_rows, src_rows, dst_rows, cot_rows = block_rows
        mem_src = jnp.take(memory, src_rows, axis=0)
        mem_dst = jnp.take(memory, dst_rows, axis=0)
        d_source, d_target, saved_rows = event_backward(mem_src, mem_dst, edge_rows, cot_rows, w_first, w_second, w_input, w_hidden)
        inputs, d_pre, hidden, d_message, message, d_gate_in, d_gate_mem = saved_rows
        mem_grad = mem_grad.at[src_rows].add(d_source).at[dst_rows].add(d_target)
        grad_first = grad_first + jnp.dot(inputs.T, d_pre, preferred_element_type=jnp.float32)
        rest_terms = jnp.concatenate([jnp.dot(hidden.T, d_message, preferred_element_type=jnp.float32), jnp.dot(message.T, d_gate_in, preferred_element_type=jnp.float32), jnp.dot(mem_src.T, d_gate_mem, preferred_element_type=jnp.float32)], axis=1)
        return ((mem_grad, grad_first, grad_rest + rest_terms), None)
    initial = (jnp.zeros((ENTITIES, mem_width), jnp.float32), jnp.zeros((IN_ROWS, mem_width), jnp.float32), jnp.zeros((mem_width, 7 * mem_width), jnp.float32))
    blocks = (edge_features.reshape(BATCHES, E_DEV, EDGE), source.reshape(BATCHES, E_DEV), target.reshape(BATCHES, E_DEV), cotangent.reshape(BATCHES, E_DEV, mem_width))
    (mem_grad, grad_first, grad_rest), _ = lax.scan(scan_step, initial, blocks)
    grad_scale = 1.0 / math.sqrt(EVENTS)
    grad_first = grad_first * grad_scale
    grad_rest = grad_rest * grad_scale
    return (mem_grad, grad_first, grad_rest[:, :mem_width], grad_rest[:, mem_width:4 * mem_width], grad_rest[:, 4 * mem_width:])
```

```python
import functools
import math

import jax
import jax.numpy as jnp
from jax import lax
from jax.experimental import pallas as pl
from jax.experimental.pallas import tpu as pltpu
from jax.sharding import PartitionSpec as P

HUBS = 8
BF16 = jnp.bfloat16
F32 = jnp.float32


def contract_last(left, right):
    return lax.dot_general(left, right, (((1,), (1,)), ((), ())), preferred_element_type=F32)


def contract_first(left, right):
    return lax.dot_general(left, right, (((0,), (0,)), ((), ())), preferred_element_type=F32)


def swap_bit(value, axis, bit):
    size = lax.axis_size(axis)
    return lax.ppermute(value, axis, [(i, i ^ (1 << bit)) for i in range(size)])


def forward_gates(mem_src, mem_dst, edge_rows, cot_rows, w_first, w_second, w_input, w_hidden):
    width = mem_src.shape[1]
    inputs = jnp.concatenate([mem_src, mem_dst, edge_rows], axis=1)
    pre_hidden = jnp.dot(inputs, w_first, preferred_element_type=F32)
    hidden = jax.nn.silu(pre_hidden).astype(BF16)
    message = jnp.dot(hidden, w_second, preferred_element_type=F32).astype(BF16)
    gate_in = jnp.dot(message, w_input, preferred_element_type=F32)
    gate_mem = jnp.dot(mem_src, w_hidden, preferred_element_type=F32)
    reset_gate = jax.nn.sigmoid(gate_in[:, :width] + gate_mem[:, :width])
    update = jax.nn.sigmoid(gate_in[:, width : 2 * width] + gate_mem[:, width : 2 * width])
    mem_cand = gate_mem[:, 2 * width :]
    candidate = jnp.tanh(gate_in[:, 2 * width :] + reset_gate * mem_cand)
    upstream = cot_rows.astype(F32)
    pre_cand = upstream * (1.0 - update) * (1.0 - candidate * candidate)
    pre_reset = pre_cand * mem_cand * reset_gate * (1.0 - reset_gate)
    pre_update = upstream * (mem_src.astype(F32) - candidate) * update * (1.0 - update)
    d_gate_in = jnp.concatenate([pre_reset, pre_update, pre_cand], axis=1).astype(BF16)
    d_gate_mem = jnp.concatenate([pre_reset, pre_update, pre_cand * reset_gate], axis=1).astype(BF16)
    return inputs, pre_hidden, hidden, message, upstream * update, d_gate_in, d_gate_mem


def scatter_kernel(block, idx_ref, val_ref, out_ref):
    rows = pl.program_id(0) * block + lax.broadcasted_iota(jnp.int32, (block, idx_ref.shape[1]), 0)
    pick = jnp.where(rows == idx_ref[...], 1.0, 0.0).astype(BF16)
    out_ref[...] = jnp.dot(pick, val_ref[...], preferred_element_type=F32)


def scatter_rows(index, values, rows):
    count, width = values.shape
    block = 256
    return pl.pallas_call(
        functools.partial(scatter_kernel, block),
        out_shape=jax.ShapeDtypeStruct((rows, width), F32),
        grid=(rows // block,),
        in_specs=[
            pl.BlockSpec((1, count), lambda i: (0, 0)),
            pl.BlockSpec((count, width), lambda i: (0, 0)),
        ],
        out_specs=pl.BlockSpec((block, width), lambda i: (i, 0)),
        cost_estimate=pl.CostEstimate(
            flops=2 * rows * count * width,
            bytes_accessed=count * width * 2 + rows * width * 4,
            transcendentals=0,
        ),
    )(index.reshape(1, count), values)


def per_device(
    memory, edge_features, source, target, cotangent, w_first, w_second, w_input, w_hidden
):
    owners = lax.axis_size("ent")
    replicas = lax.axis_size("rep")
    rep = lax.axis_index("rep")
    ent = lax.axis_index("ent")
    rep_bits = replicas.bit_length() - 1
    ent_bits = owners.bit_length() - 1
    ent_rows, width = memory.shape
    events = source.shape[0]
    grad_scale = 1.0 / math.sqrt(events * owners * replicas)
    hub_req = events // 2
    nonhub = 2 * events - hub_req
    cap = 2 * nonhub // owners
    slots = cap + HUBS

    endpoints = jnp.concatenate([source, target])
    owner_of = endpoints // ent_rows
    local_row = endpoints % ent_rows
    is_hub = local_row < HUBS
    member = jnp.logical_and(
        owner_of[:, None] == jnp.arange(owners, dtype=jnp.int32)[None, :], ~is_hub[:, None]
    )
    place = jnp.arange(2 * events, dtype=jnp.int32)
    before = (place[None, :] < place[:, None]).astype(BF16)
    earlier = jnp.dot(before, member.astype(BF16), preferred_element_type=F32)
    rank = jnp.sum(jnp.where(member, earlier, 0.0), axis=1).astype(jnp.int32)
    slot = owner_of * slots + jnp.where(is_hub, cap + local_row, rank)
    chosen = slot[:, None] == jnp.arange(owners * slots, dtype=jnp.int32)[None, :]
    pick = chosen.astype(BF16)
    wanted = jnp.sum(jnp.where(chosen, local_row[:, None], 0), axis=0).reshape(owners, slots)
    wanted = wanted[:, :cap]

    asked = lax.all_to_all(wanted.reshape(owners, 1, cap), "ent", 0, 0, tiled=True)
    asked = asked.reshape(owners, cap)
    hub_ids = jnp.broadcast_to(jnp.arange(HUBS, dtype=jnp.int32)[None, :], (owners, HUBS))
    asked = jnp.concatenate([asked, hub_ids], axis=1)
    rows_of = asked.reshape(-1)[:, None] == jnp.arange(ent_rows, dtype=jnp.int32)[None, :]
    found = jnp.dot(rows_of.astype(BF16), memory, preferred_element_type=F32).astype(BF16)
    fetched = lax.all_to_all(found.reshape(owners, slots, width), "ent", 0, 0, tiled=True)
    gathered = jnp.dot(
        pick, fetched.reshape(owners * slots, width), preferred_element_type=F32
    ).astype(BF16)

    asked_all = asked[None]
    for bit in range(rep_bits):
        other = swap_bit(asked_all, "rep", bit)
        upper = (rep >> bit) & 1
        asked_all = jnp.where(
            upper == 1,
            jnp.concatenate([other, asked_all], axis=0),
            jnp.concatenate([asked_all, other], axis=0),
        )
    index = jnp.transpose(asked_all, (1, 0, 2)).reshape(-1)

    mem_src = gathered[:events]
    inputs, pre_hidden, hidden, message, direct, d_gate_in, d_gate_mem = forward_gates(
        mem_src, gathered[events:], edge_features, cotangent, w_first, w_second, w_input, w_hidden
    )
    d_message = contract_last(d_gate_in, w_input).astype(BF16)
    back_hidden = contract_last(d_message, w_second)
    sigma_pre = jax.nn.sigmoid(pre_hidden)
    d_pre = (back_hidden * sigma_pre * (1.0 + pre_hidden * (1.0 - sigma_pre))).astype(BF16)
    d_inputs = contract_last(d_pre, w_first[: 2 * width])
    d_source = direct + contract_last(d_gate_mem, w_hidden) + d_inputs[:, :width]
    end_grads = jnp.concatenate([d_source, d_inputs[:, width:]], axis=0).astype(BF16)

    part = width // replicas
    outgoing = contract_first(pick, end_grads).astype(BF16)
    outgoing = outgoing.reshape(owners, slots, replicas, part).transpose(0, 2, 1, 3)
    returned = lax.all_to_all(
        outgoing.reshape(owners * replicas, slots, part), ("ent", "rep"), 0, 0, tiled=True
    )
    memory_grad = scatter_rows(index, returned.reshape(-1, part), ent_rows)

    def quarter(pairs, which):
        pieces = []
        for left, right in pairs:
            cols = right.shape[1] // replicas
            piece = lax.dynamic_slice_in_dim(right, which * cols, cols, axis=1)
            pieces.append(
                (grad_scale * contract_first(left, piece)).reshape(owners, left.shape[1] // owners, cols)
            )
        return pieces

    def halve_rep(make):
        total = None
        pending = [jnp.int32(0)]
        flips = [0]
        arrived = None
        for bit in range(rep_bits):
            later = [f for f in range(replicas) if f & (1 << bit) and not f & ((1 << bit) - 1)]
            send = []
            for flip in later:
                value = make(rep ^ flip)
                if arrived is not None:
                    value = value + arrived[flip].astype(F32)
                send.append(value.astype(BF16))
            got = swap_bit(jnp.stack(send), "rep", bit)
            fresh = {}
            for place_, flip in enumerate(later):
                base = flip ^ (1 << bit)
                value = got[place_].astype(F32)
                if arrived is not None:
                    value = value + arrived[base]
                fresh[base] = value
            arrived = fresh
        return make(rep) + arrived[0]

    def halve_ent(value):
        for bit in range(ent_bits):
            upper = (ent >> bit) & 1
            shape = value.shape
            pairs = value.reshape((shape[0] // 2, 2) + shape[1:])
            keep = jnp.where(upper == 1, pairs[:, 1], pairs[:, 0])
            send = jnp.where(upper == 1, pairs[:, 0], pairs[:, 1]).astype(BF16)
            value = keep + swap_bit(send, "ent", bit).astype(F32)
        return value[0]

    def spread_rep(value):
        value = value.astype(BF16)[None]
        for bit in range(rep_bits):
            other = swap_bit(value, "rep", bit)
            upper = (rep >> bit) & 1
            value = jnp.where(
                upper == 1,
                jnp.concatenate([other, value], axis=0),
                jnp.concatenate([value, other], axis=0),
            )
        return value.astype(F32)

    def make_gate(which):
        return jnp.concatenate(
            quarter(((message, d_gate_in), (mem_src, d_gate_mem)), which), axis=2
        )

    def make_first(which):
        return jnp.concatenate(quarter(((inputs, d_pre), (hidden, d_message)), which), axis=1)

    gate_sum = spread_rep(halve_ent(halve_rep(make_gate)))
    first_sum = spread_rep(halve_ent(halve_rep(make_first)))

    def columns(value):
        return jnp.transpose(value, (1, 0, 2)).reshape(value.shape[1], -1)

    first_rows = inputs.shape[1] // owners
    gate_cols = 3 * width // replicas
    return (
        memory_grad,
        columns(first_sum[:, :first_rows]),
        columns(first_sum[:, first_rows:]),
        columns(gate_sum[:, :, :gate_cols]),
        columns(gate_sum[:, :, gate_cols:]),
    )


def solution(mesh):
    return jax.shard_map(
        per_device,
        mesh=mesh,
        in_specs=(
            P("ent", None),
            P(("ent", "rep"), None),
            P(("ent", "rep")),
            P(("ent", "rep")),
            P(("ent", "rep"), None),
            P(),
            P(),
            P(),
            P(),
        ),
        out_specs=(P("ent", "rep"), P("ent", None), P("ent", None), P("ent", None), P("ent", None)),
        check_vma=False,
    )
```

```python
import functools
import math

import jax
import jax.numpy as jnp
from jax import lax
from jax.experimental import pallas as pl
from jax.experimental.pallas import tpu as pltpu
from jax.sharding import PartitionSpec as P

HUBS = 8
BF16 = jnp.bfloat16
F32 = jnp.float32


def contract_last(left, right):
    return lax.dot_general(left, right, (((1,), (1,)), ((), ())), preferred_element_type=F32)


def contract_first(left, right):
    return lax.dot_general(left, right, (((0,), (0,)), ((), ())), preferred_element_type=F32)


def swap_bit(value, axis, bit):
    size = lax.axis_size(axis)
    return lax.ppermute(value, axis, [(i, i ^ (1 << bit)) for i in range(size)])


def forward_gates(mem_src, mem_dst, edge_rows, cot_rows, w_first, w_second, w_input, w_hidden):
    width = mem_src.shape[1]
    inputs = jnp.concatenate([mem_src, mem_dst, edge_rows], axis=1)
    pre_hidden = jnp.dot(inputs, w_first, preferred_element_type=F32)
    hidden = jax.nn.silu(pre_hidden).astype(BF16)
    message = jnp.dot(hidden, w_second, preferred_element_type=F32).astype(BF16)
    gate_in = jnp.dot(message, w_input, preferred_element_type=F32)
    gate_mem = jnp.dot(mem_src, w_hidden, preferred_element_type=F32)
    reset_gate = jax.nn.sigmoid(gate_in[:, :width] + gate_mem[:, :width])
    update = jax.nn.sigmoid(gate_in[:, width : 2 * width] + gate_mem[:, width : 2 * width])
    mem_cand = gate_mem[:, 2 * width :]
    candidate = jnp.tanh(gate_in[:, 2 * width :] + reset_gate * mem_cand)
    upstream = cot_rows.astype(F32)
    pre_cand = upstream * (1.0 - update) * (1.0 - candidate * candidate)
    pre_reset = pre_cand * mem_cand * reset_gate * (1.0 - reset_gate)
    pre_update = upstream * (mem_src.astype(F32) - candidate) * update * (1.0 - update)
    d_gate_in = jnp.concatenate([pre_reset, pre_update, pre_cand], axis=1).astype(BF16)
    d_gate_mem = jnp.concatenate([pre_reset, pre_update, pre_cand * reset_gate], axis=1).astype(BF16)
    return inputs, pre_hidden, hidden, message, upstream * update, d_gate_in, d_gate_mem


def scatter_kernel(low, idx_ref, idx_col_ref, val_ref, out_ref):
    count, width = val_ref.shape
    groups = out_ref.shape[0] // low
    lows = lax.broadcasted_iota(jnp.int32, (low, count), 0)
    pick = jnp.where(lows == idx_ref[...] % low, 1.0, 0.0).astype(BF16)
    group = jnp.broadcast_to(idx_col_ref[...] // low, (count, width))
    values = val_ref[...]
    zero = jnp.zeros_like(values)
    spread = jnp.concatenate([jnp.where(group == g, values, zero) for g in range(groups)], axis=1)
    total = jnp.dot(pick, spread, preferred_element_type=F32)
    for g in range(groups):
        out_ref[pl.ds(g * low, low), :] = total[:, g * width : (g + 1) * width]


def scatter_rows(index, values, rows):
    count, width = values.shape
    groups = 4
    return pl.pallas_call(
        functools.partial(scatter_kernel, rows // groups),
        out_shape=jax.ShapeDtypeStruct((rows, width), F32),
        cost_estimate=pl.CostEstimate(
            flops=2 * rows * count * width,
            bytes_accessed=count * width * 2 + rows * width * 4,
            transcendentals=0,
        ),
    )(index.reshape(1, count), index.reshape(count, 1), values)


def outgoing_kernel(slot_ref, grad_ref, out_ref):
    parts, slots, part = out_ref.shape
    count = slot_ref.shape[1]
    rows = pl.program_id(0) * slots + lax.broadcasted_iota(jnp.int32, (slots, count), 0)
    pick = jnp.where(rows == slot_ref[...], 1.0, 0.0).astype(BF16)
    total = jnp.dot(pick, grad_ref[...], preferred_element_type=F32).astype(BF16)
    for f in range(parts):
        out_ref[f] = total[:, f * part : (f + 1) * part]


def outgoing_rows(slot, grads, owners, slots, replicas):
    count, width = grads.shape
    part = width // replicas
    return pl.pallas_call(
        outgoing_kernel,
        out_shape=jax.ShapeDtypeStruct((owners * replicas, slots, part), BF16),
        grid=(owners,),
        in_specs=[
            pl.BlockSpec((1, count), lambda i: (0, 0)),
            pl.BlockSpec((count, width), lambda i: (0, 0)),
        ],
        out_specs=pl.BlockSpec((replicas, slots, part), lambda i: (i, 0, 0)),
        cost_estimate=pl.CostEstimate(
            flops=2 * owners * slots * count * width,
            bytes_accessed=(count + owners * slots) * width * 2,
            transcendentals=0,
        ),
    )(slot.reshape(1, count), grads)


def weight_kernel(scale, count, which_ref, *refs):
    out_ref = refs[-1]
    lane = out_ref.shape[-1]
    at = 0
    for pair in range(count):
        left, right = refs[2 * pair], refs[2 * pair + 1]
        product = scale * contract_first(left[...], right[...])
        for j in range(right.shape[1] // lane):
            out_ref[0, at] = product[:, j * lane : (j + 1) * lane].astype(out_ref.dtype)
            at += 1


def weight_parts(pairs, which, replicas, lane, scale, dtype):
    rows = pairs[0][0].shape[1]
    tiles = sum(right.shape[1] // replicas // lane for _, right in pairs)
    specs, args, flops = [], [], 0
    for left, right in pairs:
        cols = right.shape[1] // replicas
        specs.append(pl.BlockSpec(left.shape, lambda i, w: (0, 0)))
        specs.append(pl.BlockSpec((right.shape[0], cols), lambda i, w: (0, w[i])))
        args += [left, right]
        flops += 2 * left.shape[0] * rows * cols
    number = which.shape[0]
    return pl.pallas_call(
        functools.partial(weight_kernel, scale, len(pairs)),
        out_shape=jax.ShapeDtypeStruct((number, tiles, rows, lane), dtype),
        grid_spec=pltpu.PrefetchScalarGridSpec(
            num_scalar_prefetch=1,
            grid=(number,),
            in_specs=specs,
            out_specs=pl.BlockSpec((1, tiles, rows, lane), lambda i, w: (i, 0, 0, 0)),
        ),
        cost_estimate=pl.CostEstimate(
            flops=flops * number,
            bytes_accessed=number * tiles * rows * lane * jnp.dtype(dtype).itemsize,
            transcendentals=0,
        ),
    )(which, *args)


def per_device(
    memory, edge_features, source, target, cotangent, w_first, w_second, w_input, w_hidden
):
    owners = lax.axis_size("ent")
    replicas = lax.axis_size("rep")
    rep = lax.axis_index("rep")
    ent = lax.axis_index("ent")
    rep_bits = replicas.bit_length() - 1
    ent_bits = owners.bit_length() - 1
    ent_rows, width = memory.shape
    events = source.shape[0]
    grad_scale = 1.0 / math.sqrt(events * owners * replicas)
    hub_req = events // 2
    nonhub = 2 * events - hub_req
    cap = 2 * nonhub // owners
    slots = cap + HUBS

    endpoints = jnp.concatenate([source, target])
    owner_of = endpoints // ent_rows
    local_row = endpoints % ent_rows
    is_hub = local_row < HUBS
    member = jnp.logical_and(
        owner_of[:, None] == jnp.arange(owners, dtype=jnp.int32)[None, :], ~is_hub[:, None]
    )
    place = jnp.arange(2 * events, dtype=jnp.int32)
    before = (place[None, :] < place[:, None]).astype(BF16)
    earlier = jnp.dot(before, member.astype(BF16), preferred_element_type=F32)
    rank = jnp.sum(jnp.where(member, earlier, 0.0), axis=1).astype(jnp.int32)
    slot = owner_of * slots + jnp.where(is_hub, cap + local_row, rank)
    chosen = slot[:, None] == jnp.arange(owners * slots, dtype=jnp.int32)[None, :]
    pick = chosen.astype(BF16)
    wanted = jnp.sum(jnp.where(chosen, local_row[:, None], 0), axis=0).reshape(owners, slots)
    wanted = wanted[:, :cap]

    asked = lax.all_to_all(wanted.reshape(owners, 1, cap), "ent", 0, 0, tiled=True)
    asked = asked.reshape(owners, cap)
    hub_ids = jnp.broadcast_to(jnp.arange(HUBS, dtype=jnp.int32)[None, :], (owners, HUBS))
    asked = jnp.concatenate([asked, hub_ids], axis=1)
    rows_of = asked.reshape(-1)[:, None] == jnp.arange(ent_rows, dtype=jnp.int32)[None, :]
    found = jnp.dot(rows_of.astype(BF16), memory, preferred_element_type=F32).astype(BF16)
    fetched = lax.all_to_all(found.reshape(owners, slots, width), "ent", 0, 0, tiled=True)
    gathered = jnp.dot(
        pick, fetched.reshape(owners * slots, width), preferred_element_type=F32
    ).astype(BF16)

    asked_all = asked[None]
    for bit in range(rep_bits):
        other = swap_bit(asked_all, "rep", bit)
        upper = (rep >> bit) & 1
        asked_all = jnp.where(
            upper == 1,
            jnp.concatenate([other, asked_all], axis=0),
            jnp.concatenate([asked_all, other], axis=0),
        )
    index = jnp.transpose(asked_all, (1, 0, 2)).reshape(-1)

    mem_src = gathered[:events]
    inputs, pre_hidden, hidden, message, direct, d_gate_in, d_gate_mem = forward_gates(
        mem_src, gathered[events:], edge_features, cotangent, w_first, w_second, w_input, w_hidden
    )
    d_message = contract_last(d_gate_in, w_input).astype(BF16)
    back_hidden = contract_last(d_message, w_second)
    sigma_pre = jax.nn.sigmoid(pre_hidden)
    d_pre = (back_hidden * sigma_pre * (1.0 + pre_hidden * (1.0 - sigma_pre))).astype(BF16)
    d_inputs = contract_last(d_pre, w_first[: 2 * width])
    d_source = direct + contract_last(d_gate_mem, w_hidden) + d_inputs[:, :width]
    end_grads = jnp.concatenate([d_source, d_inputs[:, width:]], axis=0).astype(BF16)

    part = width // replicas
    outgoing = outgoing_rows(slot, end_grads, owners, slots, replicas)
    outgoing, d_message, d_pre = lax.optimization_barrier((outgoing, d_message, d_pre))
    returned = lax.all_to_all(outgoing, ("ent", "rep"), 0, 0, tiled=True)
    memory_grad = scatter_rows(index, returned.reshape(-1, width // replicas), ent_rows)

    keep_first = [f for f in range(replicas) if not f & 1]
    mine = rep ^ jnp.array(keep_first, jnp.int32)

    def start(pairs):
        send = weight_parts(pairs, mine ^ 1, replicas, part, grad_scale, BF16)
        return swap_bit(send, "rep", 0)

    def finish(pairs, arrived, order):
        value = weight_parts(pairs, mine, replicas, part, grad_scale, F32) + arrived.astype(F32)
        number, tiles, rows, lane = value.shape
        value = value.reshape((2,) * (rep_bits - 1) + (tiles,) + (2,) * ent_bits + (rows // owners, lane))
        left_rep = list(range(rep_bits - 1, 0, -1))
        left_ent = list(range(ent_bits - 1, -1, -1))
        for axis, bit in order:
            if axis == "rep":
                dim = left_rep.index(bit)
                left_rep.remove(bit)
                keep_at, send_at = jnp.int32(0), jnp.int32(1)
            else:
                dim = len(left_rep) + 1 + left_ent.index(bit)
                left_ent.remove(bit)
                keep_at = (ent >> bit) & 1
                send_at = 1 - keep_at
            send = lax.dynamic_index_in_dim(value, send_at, dim, keepdims=False).astype(BF16)
            keep = lax.dynamic_index_in_dim(value, keep_at, dim, keepdims=False)
            value = keep + swap_bit(send, axis, bit).astype(F32)
        return value.reshape(-1, lane)

    def rest(axis, bits, taken):
        return [(axis, b) for b in range(bits) if (axis, b) not in taken]

    def order_of(*head):
        taken = set(head) | {("rep", 0)}
        return list(head) + rest("rep", rep_bits, taken) + rest("ent", ent_bits, taken)

    pairs_in = ((message, d_gate_in),)
    pairs_mem = ((mem_src, d_gate_mem), (hidden, d_message))
    pairs_first = ((inputs, d_pre),)
    arrived_in = start(pairs_in)
    arrived_mem = start(pairs_mem)
    arrived_first = start(pairs_first)
    sum_in = finish(pairs_in, arrived_in, order_of(("rep", rep_bits - 1)))
    sum_mem = finish(pairs_mem, arrived_mem, order_of(("ent", 0)))
    sum_first = finish(pairs_first, arrived_first, order_of(("ent", 1)))

    value = jnp.concatenate([sum_first, sum_mem, sum_in], axis=0).astype(BF16)[None]
    for bit in range(rep_bits - 1, -1, -1):
        other = swap_bit(value, "rep", bit)
        upper = (rep >> bit) & 1
        pair = jnp.where(upper == 1, jnp.stack([other, value]), jnp.stack([value, other]))
        value = pair.reshape((-1,) + value.shape[1:])
    lane = value.shape[-1]
    value = value.reshape((2,) * rep_bits + value.shape[1:])
    value = jnp.transpose(value, tuple(range(rep_bits - 1, -1, -1)) + (rep_bits, rep_bits + 1))
    value = value.reshape((replicas,) + value.shape[rep_bits:]).astype(F32)
    first_rows = inputs.shape[1] // owners
    rows = width // owners

    def columns(at, tiles, height):
        block = value[:, at : at + tiles * height].reshape(replicas, tiles, height, lane)
        return jnp.transpose(block, (2, 0, 1, 3)).reshape(height, replicas * tiles * lane)

    tiles = 3 * width // replicas // lane
    small = width // replicas // lane
    return (
        memory_grad,
        columns(0, small, first_rows),
        columns(first_rows * small + tiles * rows, small, rows),
        columns(first_rows * small + (tiles + small) * rows, tiles, rows),
        columns(first_rows * small, tiles, rows),
    )


def solution(mesh):
    return jax.shard_map(
        per_device,
        mesh=mesh,
        in_specs=(
            P("ent", None),
            P(("ent", "rep"), None),
            P(("ent", "rep")),
            P(("ent", "rep")),
            P(("ent", "rep"), None),
            P(),
            P(),
            P(),
            P(),
        ),
        out_specs=(P("ent", "rep"), P("ent", None), P("ent", None), P("ent", None), P("ent", None)),
        check_vma=False,
    )
```

```python
import functools
import math

import jax
import jax.numpy as jnp
from jax import lax
from jax.experimental import pallas as pl
from jax.experimental.pallas import tpu as pltpu
from jax.sharding import PartitionSpec as P


HUBS = 8
FORWARD_MIB = 20
BACKWARD_MIB = 12
BF16 = jnp.bfloat16
F32 = jnp.float32


def contract_last(left, right):
    return lax.dot_general(left, right, (((1,), (1,)), ((), ())), preferred_element_type=F32)


def contract_first(left, right):
    return lax.dot_general(left, right, (((0,), (0,)), ((), ())), preferred_element_type=F32)


def swap_bit(value, axis, bit):
    size = lax.axis_size(axis)
    return lax.ppermute(value, axis, [(i, i ^ (1 << bit)) for i in range(size)])


def row_blocks(rows, block, body):
    def turn(i, carry):
        body(pl.ds(pl.multiple_of(i * block, block), block))
        return carry

    lax.fori_loop(0, rows // block, turn, 0)


def forward_kernel(
    slot_rows_ref, rows_in, edge_in, cot_in, w_first_in, w_second_in, w_input_in, w_hidden_in,
    src_ref, dst_ref, edge_ref, hidden_ref, message_ref, factor_ref, direct_ref,
    reset_ref, update_ref, cand_ref, rc_ref, d_message_ref,
    w_first_ref, w_second_ref, w_hidden_ref,
    rows_ref, cot_ref, w_input_ref, pick_ref, pre_ref, gate_in_ref, gate_mem_ref, sems,
):
    arrays = (
        (rows_in, rows_ref), (w_first_in, w_first_ref), (edge_in, edge_ref), (w_hidden_in, w_hidden_ref),
        (w_second_in, w_second_ref), (w_input_in, w_input_ref), (cot_in, cot_ref),
    )
    copies = [pltpu.make_async_copy(a, b, sems.at[i]) for i, (a, b) in enumerate(arrays)]
    for copy in copies:
        copy.start()
    events, width = src_ref.shape
    lane, total = slot_rows_ref.shape[1], rows_ref.shape[0]
    turned = jnp.transpose(slot_rows_ref[...])
    lanes = lax.broadcasted_iota(jnp.int32, (lane, total), 1)
    for k in range(2 * events // lane):
        chosen = jnp.broadcast_to(turned[:, k : k + 1], lanes.shape) == lanes
        pick_ref[k * lane : (k + 1) * lane, :] = jnp.where(chosen, 1.0, 0.0).astype(BF16)
    copies[0].wait()
    src_ref[...] = jnp.dot(pick_ref[:events, :], rows_ref[...], preferred_element_type=F32).astype(BF16)
    dst_ref[...] = jnp.dot(pick_ref[events:, :], rows_ref[...], preferred_element_type=F32).astype(BF16)
    copies[1].wait()
    copies[2].wait()
    pre_ref[...] = (
        jnp.dot(src_ref[...], w_first_ref[:width, :], preferred_element_type=F32)
        + jnp.dot(dst_ref[...], w_first_ref[width : 2 * width, :], preferred_element_type=F32)
        + jnp.dot(edge_ref[...], w_first_ref[2 * width :, :], preferred_element_type=F32)
    )

    def activate(rows):
        pre = pre_ref[rows, :]
        sigma = jax.nn.sigmoid(pre)
        hidden_ref[rows, :] = (pre * sigma).astype(BF16)
        factor_ref[rows, :] = sigma * (1.0 + pre * (1.0 - sigma))

    row_blocks(events, 32, activate)
    copies[3].wait()
    gate_mem_ref[...] = jnp.dot(src_ref[...], w_hidden_ref[...], preferred_element_type=F32)
    copies[4].wait()
    message_ref[...] = jnp.dot(hidden_ref[...], w_second_ref[...], preferred_element_type=F32).astype(BF16)
    copies[5].wait()
    gate_in_ref[...] = jnp.dot(message_ref[...], w_input_ref[...], preferred_element_type=F32)
    copies[6].wait()

    def gates(rows):
        reset = jax.nn.sigmoid(gate_in_ref[rows, :width] + gate_mem_ref[rows, :width])
        update = jax.nn.sigmoid(
            gate_in_ref[rows, width : 2 * width] + gate_mem_ref[rows, width : 2 * width]
        )
        mem_cand = gate_mem_ref[rows, 2 * width :]
        candidate = jnp.tanh(gate_in_ref[rows, 2 * width :] + reset * mem_cand)
        upstream = cot_ref[rows, :].astype(F32)
        pre_cand = upstream * (1.0 - update) * (1.0 - candidate * candidate)
        reset_ref[rows, :] = (pre_cand * mem_cand * reset * (1.0 - reset)).astype(BF16)
        update_ref[rows, :] = (
            upstream * (src_ref[rows, :].astype(F32) - candidate) * update * (1.0 - update)
        ).astype(BF16)
        cand_ref[rows, :] = pre_cand.astype(BF16)
        rc_ref[rows, :] = (pre_cand * reset).astype(BF16)
        direct_ref[rows, :] = upstream * update

    row_blocks(events, 16, gates)
    d_message_ref[...] = (
        contract_last(reset_ref[...], w_input_ref[:, :width])
        + contract_last(update_ref[...], w_input_ref[:, width : 2 * width])
        + contract_last(cand_ref[...], w_input_ref[:, 2 * width :])
    ).astype(BF16)


def off_chip(array):
    return pltpu.with_memory_space_constraint(array, pltpu.HBM)


def forward_rows(slot, rows, edge, cot, w_first, w_second, w_input, w_hidden):
    events, width = cot.shape
    lane = 128
    half = jax.ShapeDtypeStruct((events, width), BF16)
    full = jax.ShapeDtypeStruct((events, width), F32)
    like = lambda x: jax.ShapeDtypeStruct(x.shape, x.dtype)
    return pl.pallas_call(
        forward_kernel,
        out_shape=(
            half, half, like(edge), half, half, full, full, half, half, half, half, half,
            like(w_first), like(w_second), like(w_hidden),
        ),
        in_specs=[pl.BlockSpec(memory_space=pltpu.VMEM)] + [pl.BlockSpec(memory_space=pltpu.HBM)] * 7,
        out_specs=[pl.BlockSpec(memory_space=pltpu.VMEM)] * 15,
        scratch_shapes=[
            pltpu.VMEM(rows.shape, BF16),
            pltpu.VMEM(cot.shape, BF16),
            pltpu.VMEM(w_input.shape, BF16),
            pltpu.VMEM((2 * events, rows.shape[0]), BF16),
            pltpu.VMEM((events, width), F32),
            pltpu.VMEM((events, 3 * width), F32),
            pltpu.VMEM((events, 3 * width), F32),
            pltpu.SemaphoreType.DMA((7,)),
        ],
        compiler_params=pltpu.CompilerParams(vmem_limit_bytes=FORWARD_MIB << 20),
        cost_estimate=pl.CostEstimate(
            flops=2 * events * width * (2 * rows.shape[0] + 11 * width + edge.shape[1]),
            bytes_accessed=30 * events * width,
            transcendentals=4 * events * width,
        ),
    )(slot.reshape(2 * events // lane, lane), *map(off_chip, (rows, edge, cot, w_first, w_second, w_input, w_hidden)))


def backward_kernel(
    d_message_ref, factor_ref, direct_ref, reset_ref, update_ref, rc_ref, slot_ref,
    w_first_ref, w_second_ref, w_hidden_ref, d_pre_ref, away_ref, ends_ref, out_ref, sems,
):
    events, width = d_pre_ref.shape
    owners, parts, slots, part = out_ref.shape
    back = contract_last(d_message_ref[...], w_second_ref[...])
    d_pre_ref[...] = (back * factor_ref[...]).astype(BF16)
    ends_ref[:events, :] = (
        direct_ref[...]
        + contract_last(reset_ref[...], w_hidden_ref[:, :width])
        + contract_last(update_ref[...], w_hidden_ref[:, width : 2 * width])
        + contract_last(rc_ref[...], w_hidden_ref[:, 2 * width :])
        + contract_last(d_pre_ref[...], w_first_ref[:width, :])
    ).astype(BF16)
    ends_ref[events:, :] = contract_last(d_pre_ref[...], w_first_ref[width : 2 * width, :]).astype(BF16)
    half = owners // 2
    copies = []
    for h in range(2):
        rows = h * half * slots + lax.broadcasted_iota(jnp.int32, (half * slots, 2 * events), 0)
        turned = jnp.where(rows == slot_ref[...], 1.0, 0.0).astype(BF16)
        sums = jnp.dot(turned, ends_ref[...], preferred_element_type=F32).astype(BF16)
        for o in range(half):
            for f in range(parts):
                out_ref[h * half + o, f] = sums[o * slots : (o + 1) * slots, f * part : (f + 1) * part]
        here = pl.ds(h * half, half)
        copies.append(pltpu.make_async_copy(out_ref.at[here], away_ref.at[here], sems.at[h]))
        copies[-1].start()
    for copy in copies:
        copy.wait()


def backward_rows(made, slot, w_first, w_second, w_hidden, owners, slots, replicas):
    events, width = made[0].shape
    part = width // replicas
    d_pre, sums = pl.pallas_call(
        backward_kernel,
        out_shape=(
            jax.ShapeDtypeStruct((events, width), BF16),
            pltpu.HBM((owners, replicas, slots, part), BF16),
        ),
        in_specs=[pl.BlockSpec(memory_space=pltpu.VMEM)] * (len(made) + 4),
        out_specs=[pl.BlockSpec(memory_space=pltpu.VMEM), pl.BlockSpec(memory_space=pltpu.HBM)],
        scratch_shapes=[
            pltpu.VMEM((2 * events, width), BF16),
            pltpu.VMEM((owners, replicas, slots, part), BF16),
            pltpu.SemaphoreType.DMA((2,)),
        ],
        compiler_params=pltpu.CompilerParams(vmem_limit_bytes=BACKWARD_MIB << 20),
        cost_estimate=pl.CostEstimate(
            flops=2 * events * width * (2 * owners * slots + 6 * width),
            bytes_accessed=20 * events * width,
            transcendentals=0,
        ),
    )(*made, slot.reshape(1, 2 * events), w_first, w_second, w_hidden)
    return d_pre, sums.reshape(owners * replicas, slots, part)


def slots_kernel(ent_rows, slots, source_in, target_in, slot_ref, wanted_ref, source_ref, target_ref, sems):
    owners, _, cap = wanted_ref.shape
    events = source_ref.shape[0]
    copies = [
        pltpu.make_async_copy(source_in, source_ref, sems.at[0]),
        pltpu.make_async_copy(target_in, target_ref, sems.at[1]),
    ]
    for copy in copies:
        copy.start()
    for copy in copies:
        copy.wait()
    ends = jnp.concatenate(
        [source_ref[...].reshape(1, events), target_ref[...].reshape(1, events)], axis=1
    )
    count = ends.shape[1]
    owner = lax.div(ends, jnp.int32(ent_rows))
    local = ends - owner * ent_rows
    is_hub = local < HUBS
    ids = lax.broadcasted_iota(jnp.int32, (owners, count), 0)
    member = jnp.logical_and(ids == owner, jnp.logical_not(is_hub))
    total = member.astype(jnp.int32)
    lanes = lax.broadcasted_iota(jnp.int32, (owners, count), 1)
    shift = 1
    while shift < count:
        total = total + jnp.where(lanes >= shift, pltpu.roll(total, shift, 1), 0)
        shift *= 2
    rank = jnp.sum(jnp.where(member, total - 1, 0), axis=0, keepdims=True)
    slot_ref[...] = owner * slots + jnp.where(is_hub, cap + local, rank)
    places = lax.broadcasted_iota(jnp.int32, (cap, count), 0)
    taken = jnp.where(places == rank, 1.0, 0.0).astype(BF16)
    high = jnp.where(member, local // 64, 0).astype(F32).astype(BF16)
    low = jnp.where(member, local % 64, 0).astype(F32).astype(BF16)
    row = 64.0 * contract_last(high, taken) + contract_last(low, taken)
    row = row.astype(jnp.int32)
    for o in range(owners):
        wanted_ref[o] = row[o : o + 1, :]


def assign_slots(source, target, owners, cap, ent_rows):
    events = source.shape[0]
    return pl.pallas_call(
        functools.partial(slots_kernel, ent_rows, cap + HUBS),
        out_shape=(
            jax.ShapeDtypeStruct((1, 2 * events), jnp.int32),
            jax.ShapeDtypeStruct((owners, 1, cap), jnp.int32),
        ),
        in_specs=[pl.BlockSpec(memory_space=pltpu.HBM)] * 2,
        scratch_shapes=[
            pltpu.VMEM((events,), jnp.int32),
            pltpu.VMEM((events,), jnp.int32),
            pltpu.SemaphoreType.DMA((2,)),
        ],
        compiler_params=pltpu.CompilerParams(vmem_limit_bytes=6 << 20),
    )(off_chip(source), off_chip(target))


def scatter_half(low, first, idx_rows_ref, val_ref, pick_ref, out_ref, spread_ref, sums_ref, sem):
    count, width = val_ref.shape
    groups = sums_ref.shape[0] // low
    lane = idx_rows_ref.shape[1]
    group = lax.div(jnp.transpose(idx_rows_ref[...]), jnp.int32(low)) - first
    for k in range(count // lane):
        values = val_ref[k * lane : (k + 1) * lane, :]
        zero = jnp.zeros_like(values)
        own = jnp.broadcast_to(group[:, k : k + 1], values.shape)
        for g in range(groups):
            spread_ref[k * lane : (k + 1) * lane, g * width : (g + 1) * width] = jnp.where(
                own == g, values, zero
            )
    total = jnp.dot(pick_ref[...], spread_ref[...], preferred_element_type=F32)
    for g in range(groups):
        sums_ref[pl.ds(g * low, low), :] = total[:, g * width : (g + 1) * width]
    copy = pltpu.make_async_copy(sums_ref, out_ref.at[pl.ds(first * low, groups * low), :], sem)
    copy.start()
    copy.wait()


def scatter_first_kernel(
    low, idx_ref, idx_rows_ref, val_in, out_ref, pick_ref, val_ref, spread_ref, sums_ref, sems
):
    arrive = pltpu.make_async_copy(val_in, val_ref, sems.at[1])
    arrive.start()
    row = lax.rem(idx_ref[...], jnp.int32(low))

    def choose(rows):
        lows = rows.start + lax.broadcasted_iota(jnp.int32, (rows.size, row.shape[1]), 0)
        pick_ref[rows, :] = jnp.where(lows == row, 1.0, 0.0).astype(BF16)

    row_blocks(low, 16, choose)
    arrive.wait()
    scatter_half(low, 0, idx_rows_ref, val_ref, pick_ref, out_ref, spread_ref, sums_ref, sems.at[0])


def scatter_second_kernel(
    low, first, idx_rows_ref, val_ref, pick_ref, partly_ref, out_ref, spread_ref, sums_ref, sem
):
    scatter_half(low, first, idx_rows_ref, val_ref, pick_ref, out_ref, spread_ref, sums_ref, sem)


def scatter_rows(index, values, rows):
    count, width = values.shape
    groups, lane = 2, 128
    low = rows // (2 * groups)
    out = jax.ShapeDtypeStruct((rows, width), F32)
    vmem, anywhere = pl.BlockSpec(memory_space=pltpu.VMEM), pl.BlockSpec(memory_space=pl.ANY)
    scratch = [pltpu.VMEM((count, groups * width), BF16), pltpu.VMEM((groups * low, width), F32)]
    params = pltpu.CompilerParams(vmem_limit_bytes=10 << 20)
    cost = pl.CostEstimate(
        flops=rows * count * width, bytes_accessed=count * width * 2 + rows * width * 2, transcendentals=0
    )
    idx_rows = index.reshape(count // lane, lane)
    partly, pick, values = pl.pallas_call(
        functools.partial(scatter_first_kernel, low),
        out_shape=(
            out,
            jax.ShapeDtypeStruct((low, count), BF16),
            jax.ShapeDtypeStruct((count, width), BF16),
        ),
        in_specs=[vmem, vmem, anywhere],
        out_specs=[anywhere, vmem, vmem],
        scratch_shapes=scratch + [pltpu.SemaphoreType.DMA((2,))],
        compiler_params=params,
        cost_estimate=cost,
    )(index.reshape(1, count), idx_rows, values)
    return pl.pallas_call(
        functools.partial(scatter_second_kernel, low, groups),
        out_shape=out,
        in_specs=[vmem, vmem, vmem, anywhere],
        out_specs=anywhere,
        scratch_shapes=scratch + [pltpu.SemaphoreType.DMA],
        input_output_aliases={3: 0},
        compiler_params=params,
        cost_estimate=cost,
    )(idx_rows, values, pick, partly)


def halve(pairs, segments, bit, send_ref, keep_ref, sent=lambda: None):
    for mine in (False, True):
        at = 0
        for source, base, count, block in segments:
            keep, got = pairs[source]
            for p in range(count):
                row = base + (2 * p + (bit if mine else 1 - bit)) * block
                if not isinstance(bit, int):
                    row = pl.multiple_of(row, 16)
                rows = pl.ds(row, block)
                total = keep[rows, :] + got[rows, :].astype(F32)
                if mine:
                    keep_ref[pl.ds(at, block), :] = total
                else:
                    send_ref[pl.ds(at, block), :] = total.astype(BF16)
                at += block
        if not mine:
            sent()


def halve_arrays(pairs, segments, bit):
    sends, keeps = [], []
    for source, base, count, block in segments:
        keep, got = pairs[source]
        value = (keep + got.astype(F32))[base : base + 2 * count * block]
        value = value.reshape(count, 2, block, value.shape[1])
        keeps.append(lax.dynamic_index_in_dim(value, bit, 1, keepdims=False).reshape(count * block, -1))
        sends.append(lax.dynamic_index_in_dim(value, 1 - bit, 1, keepdims=False).reshape(count * block, -1))
    return jnp.concatenate(sends).astype(BF16), jnp.concatenate(keeps)


def half_shapes(segments, lane):
    rows = sum(count * block for _, _, count, block in segments)
    return (jax.ShapeDtypeStruct((rows, lane), BF16), jax.ShapeDtypeStruct((rows, lane), F32))


def bit_of(where_ref, axis, bit):
    return (where_ref[axis] >> bit) & 1


def step_kernel(number, segments, axis, bit, where_ref, *refs):
    pairs = [(refs[2 * i], refs[2 * i + 1]) for i in range(number)]
    halve(pairs, segments, 0 if axis == 0 else bit_of(where_ref, axis, bit), refs[-2], refs[-1])


def step(where, pairs, segments, axis, bit):
    if any(block % 16 for _, _, _, block in segments):
        return halve_arrays(pairs, segments, 0 if axis == 0 else (where[axis] >> bit) & 1)
    lane = pairs[0][0].shape[1]
    return pl.pallas_call(
        functools.partial(step_kernel, len(pairs), segments, axis, bit),
        compiler_params=pltpu.CompilerParams(vmem_limit_bytes=6 << 20),
        out_shape=half_shapes(segments, lane),
        in_specs=[pl.BlockSpec(memory_space=pltpu.SMEM)]
        + [pl.BlockSpec(memory_space=pltpu.VMEM)] * (2 * len(pairs)),
        cost_estimate=pl.CostEstimate(
            flops=0,
            bytes_accessed=sum(k.size * 6 for k, _ in pairs) * 2,
            transcendentals=0,
        ),
    )(where, *[x for pair in pairs for x in pair])


def write_products(scale, groups, refs, parts, lane, out_ref):
    height = out_ref.shape[0] // len(parts)
    starts = [pl.multiple_of(part * lane, lane) for part in parts]
    at = row = 0
    for lefts, rights in groups:
        pieces = [refs[at + lefts + i][:, pl.ds(start, lane)] for start in starts for i in range(rights)]
        right = jnp.concatenate(pieces, axis=1)
        for i in range(lefts):
            value = scale * contract_first(refs[at + i][...], right)
            rows = value.shape[0]
            for p in range(len(parts)):
                for t in range(rights):
                    column = (p * rights + t) * lane
                    out_ref[pl.ds(p * height + row + t * rows, rows), :] = value[
                        :, column : column + lane
                    ].astype(out_ref.dtype)
            row += rows * rights
        at += lefts + rights


def send_kernel(scale, groups, flips, where_ref, *refs):
    out_ref = refs[-1]
    parts = [where_ref[0] ^ f for f in flips]
    write_products(scale, groups, refs[:-1], parts, out_ref.shape[1], out_ref)


def keep_kernel(scale, groups, flips, segments, axis, bit, where_ref, *refs):
    *operands, got_ref, send_ref, keep_ref, sum_ref = refs
    parts = [where_ref[0] ^ f for f in flips]
    write_products(scale, groups, operands, parts, sum_ref.shape[1], sum_ref)
    which = 0 if axis == 0 else bit_of(where_ref, axis, bit)
    halve([(sum_ref, got_ref)], segments, which, send_ref, keep_ref)


def keep_away_kernel(scale, groups, flips, segments, axis, bit, where_ref, *refs):
    *operands, got_ref, send_out, keep_out, sum_ref, send_ref, keep_ref, sems = refs
    parts = [where_ref[0] ^ f for f in flips]
    lane, height = sum_ref.shape[1], sum_ref.shape[0] // len(flips)
    away = [
        pltpu.make_async_copy(send_ref, send_out, sems.at[0]),
        pltpu.make_async_copy(keep_ref, keep_out, sems.at[1]),
    ]
    if axis == 0 and len(parts) == 2:
        write_products(scale, groups, operands, parts[1:], lane, sum_ref.at[pl.ds(height, height), :])
        send_ref[...] = (sum_ref[height:, :] + got_ref[height:, :].astype(F32)).astype(BF16)
        away[0].start()
        write_products(scale, groups, operands, parts[:1], lane, sum_ref.at[pl.ds(0, height), :])
        keep_ref[...] = sum_ref[:height, :] + got_ref[:height, :].astype(F32)
    else:
        write_products(scale, groups, operands, parts, lane, sum_ref)
        which = 0 if axis == 0 else bit_of(where_ref, axis, bit)
        halve([(sum_ref, got_ref)], segments, which, send_ref, keep_ref, away[0].start)
    away[1].start()
    for copy in away:
        copy.wait()


def group_rows(groups, operands):
    rows, at = 0, 0
    for lefts, rights in groups:
        for i in range(lefts):
            rows += operands[at + i].shape[1] * rights
        at += lefts + rights
    return rows


def send_products(where, scale, groups, operands, flips, lane, dtype=BF16):
    rows = group_rows(groups, operands)
    return pl.pallas_call(
        functools.partial(send_kernel, scale, groups, flips),
        compiler_params=pltpu.CompilerParams(vmem_limit_bytes=14 << 20),
        out_shape=jax.ShapeDtypeStruct((len(flips) * rows, lane), dtype),
        in_specs=[pl.BlockSpec(memory_space=pltpu.SMEM)]
        + [pl.BlockSpec(memory_space=pltpu.VMEM)] * len(operands),
        cost_estimate=pl.CostEstimate(
            flops=2 * len(flips) * rows * lane * operands[0].shape[0],
            bytes_accessed=len(flips) * rows * lane * 2,
            transcendentals=0,
        ),
    )(where, *operands)


def keep_products(where, scale, groups, operands, flips, lane, got, segments, axis, bit, away):
    rows = group_rows(groups, operands)
    if any(block % 16 for _, _, _, block in segments):
        own = send_products(where, scale, groups, operands, flips, lane, F32)
        return halve_arrays([(own, got)], segments, 0 if axis == 0 else (where[axis] >> bit) & 1)
    send, keep = half_shapes(segments, lane)
    if away:
        return pl.pallas_call(
            functools.partial(keep_away_kernel, scale, groups, flips, segments, axis, bit),
            out_shape=(pltpu.HBM(send.shape, send.dtype), pltpu.HBM(keep.shape, keep.dtype)),
            in_specs=[pl.BlockSpec(memory_space=pltpu.SMEM)]
            + [pl.BlockSpec(memory_space=pltpu.VMEM)] * (len(operands) + 1),
            out_specs=[pl.BlockSpec(memory_space=pltpu.HBM)] * 2,
            scratch_shapes=[
                pltpu.VMEM((len(flips) * rows, lane), F32),
                pltpu.VMEM(send.shape, send.dtype),
                pltpu.VMEM(keep.shape, keep.dtype),
                pltpu.SemaphoreType.DMA((2,)),
            ],
            compiler_params=pltpu.CompilerParams(vmem_limit_bytes=18 << 20),
            cost_estimate=pl.CostEstimate(
                flops=2 * len(flips) * rows * lane * operands[0].shape[0],
                bytes_accessed=len(flips) * rows * lane * 6,
                transcendentals=0,
            ),
        )(where, *operands, got)
    return pl.pallas_call(
        functools.partial(keep_kernel, scale, groups, flips, segments, axis, bit),
        compiler_params=pltpu.CompilerParams(vmem_limit_bytes=18 << 20),
        out_shape=half_shapes(segments, lane),
        in_specs=[pl.BlockSpec(memory_space=pltpu.SMEM)]
        + [pl.BlockSpec(memory_space=pltpu.VMEM)] * (len(operands) + 1),
        scratch_shapes=[pltpu.VMEM((len(flips) * rows, lane), F32)],
        cost_estimate=pl.CostEstimate(
            flops=2 * len(flips) * rows * lane * operands[0].shape[0],
            bytes_accessed=len(flips) * rows * lane * 6,
            transcendentals=0,
        ),
    )(where, *operands, got)


def last_kernel(keep_ref, got_ref, out_ref):
    out_ref[...] = (keep_ref[...] + got_ref[...].astype(F32)).astype(BF16)


def fold_kernel(near, bit, own_ref, other_ref, out_ref):
    rows = own_ref.shape[0] // len(near)
    for i, f in enumerate(near):
        j = near.index(f ^ (1 << bit))
        total = own_ref[i * rows : (i + 1) * rows, :].astype(F32)
        total += other_ref[j * rows : (j + 1) * rows, :].astype(F32)
        out_ref[i * rows : (i + 1) * rows, :] = total.astype(BF16)


def assemble_kernel(flips, layout, where_ref, *refs):
    sources, outs = refs[: len(flips)], refs[len(flips) :]
    lane = sources[0].shape[1]
    for f, source in zip(flips, sources):
        part = where_ref[0] ^ f
        for out, column, at, height in layout:
            start = pl.multiple_of(column + part * lane, lane)
            outs[out][:, pl.ds(start, lane)] = source[pl.ds(at, height), :].astype(F32)


def assemble_first_kernel(near, where_ref, whole_ref, across_ref, out_ref):
    lane = whole_ref.shape[1]
    rows = whole_ref.shape[0] // len(near)
    for i, f in enumerate(near):
        for flip, source in ((f, whole_ref), (f ^ 1, across_ref)):
            start = pl.multiple_of((where_ref[0] ^ flip) * lane, lane)
            out_ref[:, pl.ds(start, lane)] = source[i * rows : (i + 1) * rows, :].astype(F32)


def per_device(
    memory, edge_features, source, target, cotangent, w_first, w_second, w_input, w_hidden
):
    owners = lax.axis_size("ent")
    replicas = lax.axis_size("rep")
    rep = lax.axis_index("rep")
    ent = lax.axis_index("ent")
    where = jnp.stack([rep, ent]).astype(jnp.int32)
    rep_bits = replicas.bit_length() - 1
    ent_bits = owners.bit_length() - 1
    ent_rows, width = memory.shape
    events = source.shape[0]
    grad_scale = 1.0 / math.sqrt(events * owners * replicas)
    hub_req = events // 2
    nonhub = 2 * events - hub_req
    cap = 2 * nonhub // owners
    slots = cap + HUBS

    slot, wanted = assign_slots(source, target, owners, cap, ent_rows)

    asked = lax.all_to_all(wanted, "ent", 0, 0, tiled=True)
    asked = asked.reshape(owners, cap)
    hub_ids = jnp.broadcast_to(jnp.arange(HUBS, dtype=jnp.int32)[None, :], (owners, HUBS))
    asked = jnp.concatenate([asked, hub_ids], axis=1)
    rows_of = asked.reshape(-1)[:, None] == jnp.arange(ent_rows, dtype=jnp.int32)[None, :]
    found = jnp.dot(rows_of.astype(BF16), memory, preferred_element_type=F32).astype(BF16)
    fetched = lax.all_to_all(found.reshape(owners, slots, width), "ent", 0, 0, tiled=True)
    asked_all = asked[None]
    for bit in range(rep_bits):
        other = swap_bit(asked_all, "rep", bit)
        upper = (rep >> bit) & 1
        asked_all = jnp.where(
            upper == 1,
            jnp.concatenate([other, asked_all], axis=0),
            jnp.concatenate([asked_all, other], axis=0),
        )
    index = jnp.transpose(asked_all, (1, 0, 2)).reshape(-1)

    fetched, index = lax.optimization_barrier((fetched, index))
    (
        mem_src, mem_dst, edge_rows, hidden, message, factor, direct,
        d_reset, d_update, d_cand, d_rc, d_message, w_first, w_second, w_hidden,
    ) = forward_rows(
        slot, fetched.reshape(owners * slots, width), edge_features, cotangent,
        w_first, w_second, w_input, w_hidden,
    )

    part = width // replicas
    d_pre, outgoing = backward_rows(
        (d_message, factor, direct, d_reset, d_update, d_rc),
        slot, w_first, w_second, w_hidden, owners, slots, replicas,
    )
    returned = lax.all_to_all(outgoing, ("ent", "rep"), 0, 0, tiled=True)
    returned = returned.reshape(-1, part)
    memory_grad = scatter_rows(index, returned, ent_rows)

    far = tuple(f for f in range(replicas) if f & 1)
    near = tuple(f for f in range(replicas) if not f & 1)
    rows = width // owners
    first_rows = w_first.shape[0] // owners
    chunks = {
        "in": (((1, 3),), (message, d_reset, d_update, d_cand), 3, rows),
        "mem": (((1, 3), (1, 1)), (mem_src, d_reset, d_update, d_rc, hidden, d_message), 4, rows),
        "first": (((3, 1),), (mem_src, mem_dst, edge_rows, d_pre), 1, first_rows),
    }
    dims = {
        name: [("rep", b) for b in range(rep_bits - 1, 0, -1)]
        + [("tile", chunk[2])]
        + [("ent", b) for b in range(ent_bits - 1, -1, -1)]
        for name, chunk in chunks.items()
    }

    def segment(name, source, base, which):
        sizes = [2 if d[0] != "tile" else d[1] for d in dims[name]]
        at = dims[name].index(which)
        count = math.prod(sizes[:at])
        block = math.prod(sizes[at + 1 :]) * chunks[name][3]
        dims[name].pop(at)
        return (source, base, count, block)

    def start(name):
        groups, operands, _, _ = chunks[name]
        send = send_products(where, grad_scale, groups, operands, far, part)
        return swap_bit(send, "rep", 0)

    def label(name, which):
        return f"{name}_{which[0]}{which[1]}"

    def first_step(name, got, which):
        groups, operands, _, _ = chunks[name]
        segments = (segment(name, 0, 0, which),)
        axis = 0 if which[0] == "rep" else 1
        send, keep = keep_products(
            where, grad_scale, groups, operands, near, part, got, segments, axis, which[1],
            name == "mem",
        )
        return keep, swap_bit(send, *which)

    def next_step(names, pairs, which):
        segments = []
        for source, members in enumerate(names):
            base = 0
            for name in members:
                made = segment(name, source, base, which)
                segments.append(made)
                base += 2 * made[2] * made[3]
        axis = 0 if which[0] == "rep" else 1
        name = label("_".join(sum(names, ())), which)
        send, keep = step(where, pairs, tuple(segments), axis, which[1])
        return keep, swap_bit(send, *which)

    rep_order = [("rep", b) for b in range(rep_bits - 1, 0, -1)]
    ent_order = [("ent", b) for b in range(ent_bits)]
    arrived = {name: start(name) for name in chunks}

    def run(name, order):
        pair = first_step(name, arrived[name], order[0])
        for which in order[1:]:
            pair = next_step(((name,),), (pair,), which)
        return pair

    pair_in = run("in", ent_order[:1] + rep_order)
    pair_mem = run("mem", rep_order + ent_order[:1])
    pair_both = next_step((("in",), ("mem",)), (pair_in, pair_mem), ent_order[1])
    for which in ent_order[2:]:
        pair_both = next_step((("in", "mem"),), (pair_both,), which)
    pair_first = run("first", ent_order)

    def rounded(pair):
        return pl.pallas_call(
            last_kernel,
            out_shape=jax.ShapeDtypeStruct(pair[0].shape, BF16),
            compiler_params=pltpu.CompilerParams(vmem_limit_bytes=4 << 20),
        )(*pair)

    shards = {0: rounded(pair_both)}
    for bit in range(rep_bits - 1, -1, -1):
        for f in sorted(shards):
            shards[f | 1 << bit] = swap_bit(shards[f], "rep", bit)
    flips = tuple(sorted(shards))

    whole = rounded(pair_first)
    for bit in range(rep_bits - 1, 0, -1):
        other = swap_bit(whole, "rep", bit)
        whole = pl.pallas_call(
            functools.partial(fold_kernel, near, bit),
            out_shape=jax.ShapeDtypeStruct(whole.shape, BF16),
            compiler_params=pltpu.CompilerParams(vmem_limit_bytes=4 << 20),
        )(whole, other)
    across = swap_bit(whole, "rep", 0)

    at_mem = 3 * rows
    layout = [(1, t * width, t * rows, rows) for t in range(3)]
    layout += [(2, t * width, at_mem + t * rows, rows) for t in range(3)]
    layout += [(0, 0, at_mem + 3 * rows, rows)]
    smem, vmem = pl.BlockSpec(memory_space=pltpu.SMEM), pl.BlockSpec(memory_space=pltpu.VMEM)
    second_grad, input_grad, hidden_grad = pl.pallas_call(
        functools.partial(assemble_kernel, flips, tuple(layout)),
        compiler_params=pltpu.CompilerParams(vmem_limit_bytes=6 << 20),
        out_shape=(
            jax.ShapeDtypeStruct((rows, width), F32),
            jax.ShapeDtypeStruct((rows, 3 * width), F32),
            jax.ShapeDtypeStruct((rows, 3 * width), F32),
        ),
        in_specs=[smem] + [vmem] * len(flips),
    )(where, *[shards[f] for f in flips])
    first_grad = pl.pallas_call(
        functools.partial(assemble_first_kernel, near),
        compiler_params=pltpu.CompilerParams(vmem_limit_bytes=4 << 20),
        out_shape=jax.ShapeDtypeStruct((first_rows, width), F32),
        in_specs=[smem, vmem, vmem],
    )(where, whole, across)
    return memory_grad, first_grad, second_grad, input_grad, hidden_grad


def solution(mesh):
    return jax.shard_map(
        per_device,
        mesh=mesh,
        in_specs=(
            P("ent", None),
            P(("ent", "rep"), None),
            P(("ent", "rep")),
            P(("ent", "rep")),
            P(("ent", "rep"), None),
            P(),
            P(),
            P(),
            P(),
        ),
        out_specs=(P("ent", "rep"), P("ent", None), P("ent", None), P("ent", None), P("ent", None)),
        check_vma=False,
    )
```
